1024 devices in a mesh: latent: 64 (over x_lo, z, core), blk: 16 (over y, x_hi).
Axes of the slice: x: 4 (x_hi: 2, x_lo: 2; x = x_hi * 2 + x_lo), y: 8, z: 16, core: 2. Of those that a mesh axis runs over, the one named last changes fastest.
Arguments:
- activations: bfloat16 [131072, 8192], P(('latent', 'blk')), may hold values from -90 to 90
- block_ids: int32 [131072, 1], P(('latent', 'blk')), may hold values from 0 to 63; in each aligned block of 128 rows (0 to 127, 128 to 255, ...) at most 2 rows name the same one
- enc_weight: bfloat16 [64, 8192, 128], P('latent'), may hold values from -0.0625 to 0.0625
- enc_bias: float32 [64, 128], P('latent'), may hold values from -3 to 3
- dec_weight: bfloat16 [64, 128, 8192], P('latent'), may hold values from -0.5 to 0.5
- dec_bias: float32 [8192], replicated, may hold values from -5 to 5
Outputs:
- recon_loss: float32 [], replicated
- latent_codes: bfloat16 [131072, 128], P(('latent', 'blk'))
- dec_weight_grad: float32 [64, 128, 8192], P('latent', None, 'blk')
The draws below stay inside these ranges and needn't reach their ends.
Inputs may be any that keep to these rules, and one draw needn't show every extreme that they name: `block_ids`: among the rows of one device, every block number is named by exactly 2 rows.
All inputs are finite; a program needn't handle non-finite values.
Results may differ from the reference program's by a relative error of at most 0.0095.
Values may be sent and summed in bfloat16 or wider, within the bound.
No kernel may reach another device: no remote copies, remote signals or barrier semaphores. Data moves between devices by JAX's collectives and lax.ppermute only.
A program may use at most 64 MiB of HBM per device.

```python
import math
import jax
import jax.numpy as jnp
import numpy as np
from jax import lax

D = 8192
BW = 128
TOK_DEV = 128
BLOCKS = 64
CAP = 2
TOKENS = 131072


def draw_activations(key, part):
    key_rows, key_cols, key_base = jax.random.split(key, 3)
    position = jnp.arange(TOKENS, dtype=jnp.float32) / TOKENS
    row_scale = 3.0 ** (0.5 * position) * 10.0 ** jax.random.uniform(key_rows, (TOKENS,), jnp.float32, -0.5, 0.5)
    col_scale = 10.0 ** jax.random.uniform(key_cols, (D,), jnp.float32, -0.5, 0.5)
    base = jnp.clip(jax.random.normal(key_base, (TOKENS, D), jnp.float32), -5.0, 5.0)
    return (base * row_scale[:, None] * col_scale[None, :]).astype(jnp.bfloat16)


def block_scale(own_key, extent, cuts, smallest, largest):
    loudness, own = 1.0, jax.random.fold_in(own_key, 6)
    for axis_at, parts in cuts:
        steps = jnp.exp(jax.random.uniform(jax.random.fold_in(own, axis_at), (parts,), jnp.float32, smallest / len(cuts), largest / len(cuts)))
        loudness = loudness * jnp.repeat(steps, extent[axis_at] // parts).reshape([-1 if axis == axis_at else 1 for axis in range(len(extent))])
    return loudness


def routed_block(stream_key, own, number, rows, amount, top, bound, skew):
    ranking = jax.random.permutation(stream_key, amount)
    packed, usual = shares(amount, rows * top, bound, skew, True), shares(amount, rows * top, bound, skew, False)
    places = jnp.arange(amount)

    def named(sizes, offset_by):
        used = int((sizes > 0).sum())
        fixed = max(1, used // 4)
        shifted = fixed + (places - fixed + offset_by * (used - fixed)) % max(1, amount - fixed)
        return jnp.zeros((amount,), jnp.int32).at[ranking[jnp.where(places < fixed, places, shifted)]].set(jnp.asarray(sizes, jnp.int32))

    sizes = jnp.where(number % 4 == 0, named(packed, number // 4), named(usual, number - number // 4 - 1))
    mixed = jax.random.permutation(jax.random.fold_in(own, 3), amount)
    giver, taker = mixed[0:amount // 2 * 2:2], mixed[1:amount // 2 * 2:2]
    slack = jnp.minimum(sizes[giver] - 1, bound - sizes[taker]) // 2
    slack = jnp.where((giver == ranking[0]) | (taker == ranking[0]) | (sizes[taker] == 0), 0, jnp.maximum(slack, 0))
    shifted = jax.random.randint(jax.random.fold_in(own, 4), (amount // 2,), 0, 1 << 20) % (slack + 1)
    sizes = sizes.at[giver].add(-shifted).at[taker].add(shifted)
    labels = jnp.searchsorted(jnp.cumsum(sizes), jnp.arange(rows * top), side="right").astype(jnp.int32)
    grid = labels.reshape(top, rows).T
    grid = grid[jax.random.permutation(jax.random.fold_in(own, 1), rows)]
    offset_by = jax.random.randint(jax.random.fold_in(own, 2), (rows, 1), 0, top)
    return jnp.take_along_axis(grid, (jnp.arange(top)[None, :] + offset_by) % top, axis=1)


def shares(number_of, total, limit, lean, full):
    loads = [(1 << 20) // math.isqrt(rank ** lean) + 1 for rank in range(1, number_of + 1)]
    largest = limit if full else min(limit, max(-(-total // number_of), total * loads[0] // sum(loads)))
    least = 1 if total - largest >= number_of - 1 else 0
    holding, spare = [largest] + [least] * (number_of - 1), total - largest - least * (number_of - 1)
    while spare > 0:
        movable = [i for i in range(1, number_of) if holding[i] < largest] or [i for i in range(1, number_of) if holding[i] < limit]
        pool, budget = sum([loads[i] for i in movable]), spare
        for i in movable:
            addition = min(limit - holding[i], max(1, budget * loads[i] // pool), spare)
            holding[i] = holding[i] + addition
            spare = spare - addition
    return np.array(holding)


def scatter_about(stream_key, shape, deviation, most, pieces=(), held_as=jnp.bfloat16):
    entries = jax.random.normal(stream_key, shape, jnp.float32) * deviation
    if len(pieces) > 0:
        entries = block_scale(stream_key, shape, pieces, -0.22, 0.18) * entries
    return jnp.clip(entries, min=-most, max=most).astype(held_as)


def setup_inputs(seed: int = 0) -> dict:
    arg_keys = jax.random.split(jax.random.key(seed), 7)
    activations = draw_activations(jax.random.fold_in(arg_keys[6], 71), 0)
    block_ids_keys = jax.random.split(jax.random.fold_in(arg_keys[1], 1), TOKENS // TOK_DEV)
    block_ids_turns = jax.random.permutation(jax.random.fold_in(arg_keys[1], 3), TOKENS // TOK_DEV)
    block_ids = jax.vmap(lambda own, number: routed_block(jax.random.fold_in(arg_keys[1], 2), own, number, TOK_DEV, BLOCKS, 1, CAP, 0))(block_ids_keys, block_ids_turns).reshape((TOKENS, 1))
    enc_weight = scatter_about(arg_keys[2], (BLOCKS, D, BW), D ** -0.5, 0.0625, ((0, 64),))
    enc_bias = scatter_about(arg_keys[3], (BLOCKS, BW), 0.5, 3.0, ((0, 64),), jnp.float32)
    dec_weight = scatter_about(arg_keys[4], (BLOCKS, BW, D), BW ** -0.5, 0.5, ((0, 64),))
    dec_bias = scatter_about(arg_keys[5], (D,), 1.0, 5.0, (), jnp.float32)
    return {"activations": activations, "block_ids": block_ids, "enc_weight": enc_weight, "enc_bias": enc_bias, "dec_weight": dec_weight, "dec_bias": dec_bias}


def reference(activations, block_ids, enc_weight, enc_bias, dec_weight, dec_bias):
    block_of = block_ids[:, 0]
    sorted_rows = jnp.argsort(block_of, stable=True).astype(jnp.int32)
    grouped = activations[sorted_rows].reshape(BLOCKS, TOKENS // BLOCKS, D)

    def per_block(inputs):
        rows_in, encoder, bias_in, decoder = inputs
        centered = (rows_in.astype(jnp.float32) - dec_bias).astype(jnp.bfloat16)
        pre_codes = jnp.dot(centered, encoder, preferred_element_type=jnp.float32) + bias_in
        codes = jnp.maximum(pre_codes, 0.0).astype(jnp.bfloat16)
        error_rows = jnp.dot(codes, decoder, preferred_element_type=jnp.float32) + dec_bias - rows_in.astype(jnp.float32)
        squares = jnp.sum(error_rows * error_rows)
        gradient = jnp.dot(codes.T, error_rows.astype(jnp.bfloat16), preferred_element_type=jnp.float32) / (TOKENS // BLOCKS)
        return codes, squares, gradient

    codes, squares, gradient = lax.map(per_block, (grouped, enc_weight, enc_bias, dec_weight))
    inverse = jnp.zeros((TOKENS,), jnp.int32).at[sorted_rows].set(jnp.arange(TOKENS, dtype=jnp.int32))
    latent_codes = codes.reshape(TOKENS, BW)[inverse]
    recon_loss = jnp.sum(squares) / (TOKENS * D)
    return recon_loss, latent_codes, gradient
```

```python
import jax
import jax.numpy as jnp
from jax import lax
from jax.sharding import PartitionSpec as P


def local(activations, block_ids, enc_weight, enc_bias, dec_weight, dec_bias):
    groups = lax.axis_size("latent")
    replicas = lax.axis_size("blk")
    tok_rows = activations.shape[0]
    features = activations.shape[1]
    width = enc_weight.shape[2]
    per_owner = tok_rows // groups
    block_of = block_ids[:, 0]
    matches = (block_of[:, None] == block_of[None, :]).astype(jnp.int32)
    earlier = jnp.sum(jnp.tril(matches, -1), axis=1)
    placed = block_of * per_owner + earlier
    source_row = (
        jnp.zeros((tok_rows,), jnp.int32).at[placed].set(jnp.arange(tok_rows, dtype=jnp.int32))
    )
    outgoing = activations[source_row]
    rows_block = tok_rows * replicas
    contract = (((0,), (0,)), ((), ()))
    incoming = lax.all_to_all(outgoing, "latent", split_axis=0, concat_axis=0, tiled=True)
    centered = (incoming.astype(jnp.float32) - dec_bias).astype(jnp.bfloat16)
    pre_codes = jnp.dot(centered, enc_weight[0], preferred_element_type=jnp.float32) + enc_bias[0]
    codes = jnp.maximum(pre_codes, 0.0).astype(jnp.bfloat16)
    error_rows = (
        jnp.dot(codes, dec_weight[0], preferred_element_type=jnp.float32)
        + dec_bias
        - incoming.astype(jnp.float32)
    )
    squares = jnp.sum(error_rows * error_rows)
    partial_grad = lax.dot_general(
        codes, error_rows.astype(jnp.bfloat16), contract, preferred_element_type=jnp.float32
    )
    returned, latent_parts = lax.all_to_all(
        (codes, jnp.full((groups, 1), squares, jnp.float32)),
        "latent", split_axis=0, concat_axis=0, tiled=True,
    )
    latent_sum = jnp.sum(latent_parts)
    chunks = (
        partial_grad.astype(jnp.bfloat16)
        .reshape(width, replicas, features // replicas)
        .transpose(1, 0, 2)
    )
    gathered, blk_parts = lax.all_to_all(
        (chunks, jnp.full((replicas, 1), latent_sum, jnp.float32)),
        "blk", split_axis=0, concat_axis=0, tiled=True,
    )
    summed = jnp.sum(gathered.astype(jnp.float32), axis=0)
    token_codes = returned[placed]
    gradient = summed / rows_block
    summed_loss = jnp.sum(blk_parts)
    loss_value = summed_loss / (tok_rows * groups * replicas * features)
    return (loss_value, token_codes, gradient[None])


def solution(mesh):
    placed = (
        P(("latent", "blk"), None),
        P(("latent", "blk"), None),
        P("latent", None, None),
        P("latent", None),
        P("latent", None, None),
        P(),
    )
    return jax.shard_map(
        local,
        mesh=mesh,
        in_specs=placed,
        out_specs=(P(), P(("latent", "blk"), None), P("latent", None, "blk")),
        check_vma=False,
    )
```

```python
import functools
import jax
import jax.numpy as jnp
from jax import lax
from jax.experimental import pallas as pl
from jax.experimental.pallas import tpu as pltpu
from jax.sharding import PartitionSpec as P

F32 = jnp.float32
BF16 = jnp.bfloat16


def _pieces_row(s, lanes):
    hi = s.astype(BF16).astype(F32)
    mid = (s - hi).astype(BF16).astype(F32)
    lo = s - hi - mid
    lane = lax.broadcasted_iota(jnp.int32, (1, lanes), 1)
    row = jnp.where(lane == 0, hi, jnp.where(lane == 1, mid, jnp.where(lane == 2, lo, 0.0)))
    return row.astype(BF16)


def _sae_kernel(x_ref, bias_ref, enc_ref, encb_ref, dec_ref, codes_ref, grad_ref,
                acc_s, codes_s, codes_t_s, sq_s, *, n_tiles, tile, chunk, replicas):
    p = pl.program_id(0)
    t = pl.program_id(1)

    @pl.when((p == 0) & (t == 0))
    def _():
        acc_s[...] = jnp.zeros_like(acc_s)
        sq_s[...] = jnp.zeros_like(sq_s)

    @pl.when(p == 0)
    def _():
        centered = (x_ref[...].astype(F32) - bias_ref[...]).astype(BF16)
        acc_s[...] += jnp.dot(centered, enc_ref[...], preferred_element_type=F32)

    @pl.when((p == 1) & (t == 0))
    def _():
        codes = jnp.maximum(acc_s[...] + encb_ref[...], 0.0)
        codes_s[...] = codes.astype(BF16)
        codes_t_s[...] = codes.T.astype(BF16)
        codes_ref[...] = codes.astype(BF16)

    @pl.when(p == 1)
    def _():
        err = (jnp.dot(codes_s[...], dec_ref[...], preferred_element_type=F32)
               + bias_ref[...] - x_ref[...].astype(F32))
        sq_s[...] += err * err
        g = jnp.dot(codes_t_s[...], err.astype(BF16), preferred_element_type=F32)
        per = tile // chunk
        for q in range(per):
            grad_ref[t * per + q, 0:g.shape[0], :] = g[:, q * chunk:(q + 1) * chunk].astype(BF16)

    @pl.when((p == 1) & (t == n_tiles - 1))
    def _():
        col = jnp.sum(sq_s[...], axis=0, keepdims=True)
        s = jnp.sum(col, axis=1, keepdims=True)
        row = _pieces_row(s, chunk)
        width = codes_s.shape[1]
        for q in range(replicas):
            grad_ref[q, width:width + 1, :] = row


def fused_step(x, bias, enc, encb, dec, *, replicas, tile=2048, interpret=False):
    rows, feat = x.shape
    width = enc.shape[1]
    n_tiles = feat // tile
    chunk = feat // replicas
    kernel = functools.partial(_sae_kernel, n_tiles=n_tiles, tile=tile, chunk=chunk, replicas=replicas)

    def enc_map(p, t):
        return (t * (1 - p) + (n_tiles - 1) * p, 0)

    def dec_map(p, t):
        return (0, t * p)

    return pl.pallas_call(
        kernel,
        grid=(2, n_tiles),
        in_specs=[
            pl.BlockSpec((rows, tile), lambda p, t: (0, t)),
            pl.BlockSpec((1, tile), lambda p, t: (0, t)),
            pl.BlockSpec((tile, width), enc_map),
            pl.BlockSpec((1, width), lambda p, t: (0, 0)),
            pl.BlockSpec((width, tile), dec_map),
        ],
        out_specs=[
            pl.BlockSpec((rows, width), lambda p, t: (0, 0)),
            pl.BlockSpec((replicas, width + 1, chunk), lambda p, t: (0, 0, 0)),
        ],
        out_shape=[
            jax.ShapeDtypeStruct((rows, width), BF16),
            jax.ShapeDtypeStruct((replicas, width + 1, chunk), BF16),
        ],
        scratch_shapes=[
            pltpu.VMEM((rows, width), F32),
            pltpu.VMEM((rows, width), BF16),
            pltpu.VMEM((width, rows), BF16),
            pltpu.VMEM((rows, tile), F32),
        ],
        compiler_params=pltpu.CompilerParams(
            dimension_semantics=("arbitrary", "arbitrary"),
            vmem_limit_bytes=48 * 1024 * 1024,
        ),
        interpret=interpret,
    )(x, bias.reshape(1, feat), enc, encb, dec)


def _split_pieces(s, lanes):
    hi = lax.reduce_precision(s, exponent_bits=8, mantissa_bits=7)
    mid = lax.reduce_precision(s - hi, exponent_bits=8, mantissa_bits=7)
    lo = s - hi - mid
    lane = jnp.arange(lanes)
    row = jnp.where(lane == 0, hi, jnp.where(lane == 1, mid, jnp.where(lane == 2, lo, 0.0)))
    return row.astype(BF16)


def local(activations, block_ids, enc_weight, enc_bias, dec_weight, dec_bias):
    groups = lax.axis_size("latent")
    replicas = lax.axis_size("blk")
    tok_rows = activations.shape[0]
    features = activations.shape[1]
    width = enc_weight.shape[2]
    per_owner = tok_rows // groups
    block_of = block_ids[:, 0]
    matches = (block_of[:, None] == block_of[None, :]).astype(jnp.int32)
    earlier = jnp.sum(jnp.tril(matches, -1), axis=1)
    placed = block_of * per_owner + earlier
    source_row = (
        jnp.zeros((tok_rows,), jnp.int32).at[placed].set(jnp.arange(tok_rows, dtype=jnp.int32))
    )
    outgoing = activations[source_row]
    rows_block = tok_rows * replicas
    incoming = lax.all_to_all(outgoing, "latent", split_axis=0, concat_axis=0, tiled=True)
    codes, grad_rows = fused_step(
        incoming, dec_bias, enc_weight[0], enc_bias, dec_weight[0], replicas=replicas
    )
    gathered = lax.all_to_all(grad_rows, "blk", split_axis=0, concat_axis=0, tiled=True)
    summed = jnp.sum(gathered[:, :width, :].astype(F32), axis=0)
    blk_sum = jnp.sum(jnp.sum(gathered[:, width, :3].astype(F32), axis=1))
    loss_row = jnp.broadcast_to(_split_pieces(blk_sum, width)[None, None, :], (groups, 1, width))
    sendback = jnp.concatenate([codes.reshape(groups, per_owner, width), loss_row], axis=1)
    returned = lax.all_to_all(sendback, "latent", split_axis=0, concat_axis=0, tiled=True)
    token_codes = returned[:, :per_owner, :].reshape(tok_rows, width)[placed]
    summed_loss = jnp.sum(jnp.sum(returned[:, per_owner, :3].astype(F32), axis=1))
    gradient = summed / rows_block
    loss_value = summed_loss / (tok_rows * groups * replicas * features)
    return (loss_value, token_codes, gradient[None])


def solution(mesh):
    placed = (
        P(("latent", "blk"), None),
        P(("latent", "blk"), None),
        P("latent", None, None),
        P("latent", None),
        P("latent", None, None),
        P(),
    )
    return jax.shard_map(
        local,
        mesh=mesh,
        in_specs=placed,
        out_specs=(P(), P(("latent", "blk"), None), P("latent", None, "blk")),
        check_vma=False,
    )
```

```python
import functools
import jax
import jax.numpy as jnp
from jax import lax
from jax.experimental import pallas as pl
from jax.experimental.pallas import tpu as pltpu
from jax.sharding import PartitionSpec as P

F32 = jnp.float32
BF16 = jnp.bfloat16


def _pieces_row(s, lanes):
    hi = s.astype(BF16).astype(F32)
    mid = (s - hi).astype(BF16).astype(F32)
    lo = s - hi - mid
    lane = lax.broadcasted_iota(jnp.int32, (1, lanes), 1)
    row = jnp.where(lane == 0, hi, jnp.where(lane == 1, mid, jnp.where(lane == 2, lo, 0.0)))
    return row.astype(BF16)


def _sae_kernel(x_ref, bias_ref, enc_ref, encb_ref, dec_ref, codes_ref, grad_ref,
                acc_s, codes_s, codes_t_s, sq_s, *, n_tiles, tile, chunk, replicas):
    p = pl.program_id(0)
    t = pl.program_id(1)

    @pl.when((p == 0) & (t == 0))
    def _():
        acc_s[...] = jnp.zeros_like(acc_s)
        sq_s[...] = jnp.zeros_like(sq_s)

    @pl.when(p == 0)
    def _():
        centered = (x_ref[...].astype(F32) - bias_ref[...]).astype(BF16)
        acc_s[...] += jnp.dot(centered, enc_ref[...], preferred_element_type=F32)

    @pl.when((p == 1) & (t == 0))
    def _():
        codes = jnp.maximum(acc_s[...] + encb_ref[...], 0.0)
        codes_s[...] = codes.astype(BF16)
        codes_t_s[...] = codes.T.astype(BF16)
        codes_ref[...] = codes.astype(BF16)

    @pl.when(p == 1)
    def _():
        err = (jnp.dot(codes_s[...], dec_ref[...], preferred_element_type=F32)
               + bias_ref[...] - x_ref[...].astype(F32))
        sq_s[...] += err * err
        g = jnp.dot(codes_t_s[...], err.astype(BF16), preferred_element_type=F32)
        per = tile // chunk
        for q in range(per):
            grad_ref[t * per + q, 0:g.shape[0], :] = g[:, q * chunk:(q + 1) * chunk].astype(BF16)

    @pl.when((p == 1) & (t == n_tiles - 1))
    def _():
        col = jnp.sum(sq_s[...], axis=0, keepdims=True)
        s = jnp.sum(col, axis=1, keepdims=True)
        row = _pieces_row(s, chunk)
        width = codes_s.shape[1]
        for q in range(replicas):
            grad_ref[q, width:width + 1, :] = row


def fused_step(x, bias, enc, encb, dec, *, replicas, tile=2048, interpret=False):
    rows, feat = x.shape
    width = enc.shape[1]
    n_tiles = feat // tile
    chunk = feat // replicas
    kernel = functools.partial(_sae_kernel, n_tiles=n_tiles, tile=tile, chunk=chunk, replicas=replicas)

    def enc_map(p, t):
        return (t * (1 - p) + (n_tiles - 1) * p, 0)

    def dec_map(p, t):
        return (0, t * p)

    return pl.pallas_call(
        kernel,
        grid=(2, n_tiles),
        in_specs=[
            pl.BlockSpec((rows, tile), lambda p, t: (0, t)),
            pl.BlockSpec((1, tile), lambda p, t: (0, t)),
            pl.BlockSpec((tile, width), enc_map),
            pl.BlockSpec((1, width), lambda p, t: (0, 0)),
            pl.BlockSpec((width, tile), dec_map),
        ],
        out_specs=[
            pl.BlockSpec((rows, width), lambda p, t: (0, 0)),
            pl.BlockSpec((replicas, width + 1, chunk), lambda p, t: (0, 0, 0)),
        ],
        out_shape=[
            jax.ShapeDtypeStruct((rows, width), BF16),
            jax.ShapeDtypeStruct((replicas, width + 1, chunk), BF16),
        ],
        scratch_shapes=[
            pltpu.VMEM((rows, width), F32),
            pltpu.VMEM((rows, width), BF16),
            pltpu.VMEM((width, rows), BF16),
            pltpu.VMEM((rows, tile), F32),
        ],
        compiler_params=pltpu.CompilerParams(
            dimension_semantics=("arbitrary", "arbitrary"),
            vmem_limit_bytes=48 * 1024 * 1024,
        ),
        interpret=interpret,
    )(x, bias.reshape(1, feat), enc, encb, dec)


def local(activations, block_ids, enc_weight, enc_bias, dec_weight, dec_bias):
    groups = lax.axis_size("latent")
    replicas = lax.axis_size("blk")
    tok_rows = activations.shape[0]
    features = activations.shape[1]
    width = enc_weight.shape[2]
    per_owner = tok_rows // groups
    block_of = block_ids[:, 0]
    matches = (block_of[:, None] == block_of[None, :]).astype(jnp.int32)
    earlier = jnp.sum(jnp.tril(matches, -1), axis=1)
    placed = block_of * per_owner + earlier
    source_row = (
        jnp.zeros((tok_rows,), jnp.int32).at[placed].set(jnp.arange(tok_rows, dtype=jnp.int32))
    )
    outgoing = activations[source_row]
    rows_block = tok_rows * replicas
    incoming = lax.all_to_all(outgoing, "latent", split_axis=0, concat_axis=0, tiled=True)
    codes, grad_rows = fused_step(
        incoming, dec_bias, enc_weight[0], enc_bias, dec_weight[0], replicas=replicas
    )
    gathered = lax.all_to_all(grad_rows, "blk", split_axis=0, concat_axis=0, tiled=True)
    summed = jnp.sum(gathered[:, :width, :].astype(F32), axis=0)
    blk_pieces = gathered[:, width, :3].reshape(1, 1, replicas * 3)
    loss_row = jnp.pad(blk_pieces, ((0, 0), (0, 0), (0, width - replicas * 3)))
    loss_row = jnp.broadcast_to(loss_row, (groups, 1, width))
    sendback = jnp.concatenate([codes.reshape(groups, per_owner, width), loss_row], axis=1)
    returned = lax.all_to_all(sendback, "latent", split_axis=0, concat_axis=0, tiled=True)
    token_codes = returned[:, :per_owner, :].reshape(tok_rows, width)[placed]
    summed_loss = jnp.sum(returned[:, per_owner, :].astype(F32))
    gradient = summed / rows_block
    loss_value = summed_loss / (tok_rows * groups * replicas * features)
    return (loss_value, token_codes, gradient[None])


def solution(mesh):
    placed = (
        P(("latent", "blk"), None),
        P(("latent", "blk"), None),
        P("latent", None, None),
        P("latent", None),
        P("latent", None, None),
        P(),
    )
    return jax.shard_map(
        local,
        mesh=mesh,
        in_specs=placed,
        out_specs=(P(), P(("latent", "blk"), None), P("latent", None, "blk")),
        check_vma=False,
    )
```

```python
import functools
import jax
import jax.numpy as jnp
from jax import lax
from jax.experimental import pallas as pl
from jax.experimental.pallas import tpu as pltpu
from jax.sharding import PartitionSpec as P

F32 = jnp.float32
BF16 = jnp.bfloat16


def _pieces_row(s, lanes):
    hi = s.astype(BF16).astype(F32)
    mid = (s - hi).astype(BF16).astype(F32)
    lo = s - hi - mid
    lane = lax.broadcasted_iota(jnp.int32, (1, lanes), 1)
    row = jnp.where(lane == 0, hi, jnp.where(lane == 1, mid, jnp.where(lane == 2, lo, 0.0)))
    return row.astype(BF16)


def _sae_kernel(x_ref, bias_ref, enc_ref, encb_ref, dec_ref, codes_ref, grad_ref,
                acc_s, codes_s, codes_t_s, sq_s, *, n_tiles, tile, chunk, replicas):
    p = pl.program_id(0)
    t = pl.program_id(1)

    @pl.when((p == 0) & (t == 0))
    def _():
        acc_s[...] = jnp.zeros_like(acc_s)
        sq_s[...] = jnp.zeros_like(sq_s)

    @pl.when(p == 0)
    def _():
        for h in range(2):
            centered = (x_ref[:, h, :].astype(F32) - bias_ref[...]).astype(BF16)
            acc_s[h] += jnp.dot(centered, enc_ref[...], preferred_element_type=F32)

    @pl.when((p == 1) & (t == 0))
    def _():
        for h in range(2):
            codes = jnp.maximum(acc_s[h] + encb_ref[...], 0.0)
            codes_s[h] = codes.astype(BF16)
            codes_t_s[h] = codes.T.astype(BF16)
            codes_ref[h] = codes.astype(BF16)

    @pl.when(p == 1)
    def _():
        g = None
        for h in range(2):
            err = (jnp.dot(codes_s[h], dec_ref[...], preferred_element_type=F32)
                   + bias_ref[...] - x_ref[:, h, :].astype(F32))
            sq_s[...] += err * err
            part = jnp.dot(codes_t_s[h], err.astype(BF16), preferred_element_type=F32)
            g = part if g is None else g + part
        per = tile // chunk
        for q in range(per):
            grad_ref[t * per + q, 0:g.shape[0], :] = g[:, q * chunk:(q + 1) * chunk].astype(BF16)

    @pl.when((p == 1) & (t == n_tiles - 1))
    def _():
        col = jnp.sum(sq_s[...], axis=0, keepdims=True)
        s = jnp.sum(col, axis=1, keepdims=True)
        row = _pieces_row(s, chunk)
        width = codes_s.shape[2]
        for q in range(replicas):
            grad_ref[q, width:width + 1, :] = row


def fused_step(x, bias, enc, encb, dec, *, replicas, tile=2048, interpret=False):
    groups, _, feat = x.shape
    width = enc.shape[1]
    n_tiles = feat // tile
    chunk = feat // replicas
    kernel = functools.partial(_sae_kernel, n_tiles=n_tiles, tile=tile, chunk=chunk, replicas=replicas)

    def enc_map(p, t):
        return (t * (1 - p) + (n_tiles - 1) * p, 0)

    def dec_map(p, t):
        return (0, t * p)

    return pl.pallas_call(
        kernel,
        grid=(2, n_tiles),
        in_specs=[
            pl.BlockSpec((groups, 2, tile), lambda p, t: (0, 0, t)),
            pl.BlockSpec((1, tile), lambda p, t: (0, t)),
            pl.BlockSpec((tile, width), enc_map),
            pl.BlockSpec((1, width), lambda p, t: (0, 0)),
            pl.BlockSpec((width, tile), dec_map),
        ],
        out_specs=[
            pl.BlockSpec((2, groups, width), lambda p, t: (0, 0, 0)),
            pl.BlockSpec((replicas, width + 1, chunk), lambda p, t: (0, 0, 0)),
        ],
        out_shape=[
            jax.ShapeDtypeStruct((2, groups, width), BF16),
            jax.ShapeDtypeStruct((replicas, width + 1, chunk), BF16),
        ],
        scratch_shapes=[
            pltpu.VMEM((2, groups, width), F32),
            pltpu.VMEM((2, groups, width), BF16),
            pltpu.VMEM((2, width, groups), BF16),
            pltpu.VMEM((groups, tile), F32),
        ],
        compiler_params=pltpu.CompilerParams(
            dimension_semantics=("arbitrary", "arbitrary"),
            vmem_limit_bytes=48 * 1024 * 1024,
        ),
        interpret=interpret,
    )(x, bias.reshape(1, feat), enc, encb, dec)


def local(activations, block_ids, enc_weight, enc_bias, dec_weight, dec_bias):
    groups = lax.axis_size("latent")
    replicas = lax.axis_size("blk")
    tok_rows = activations.shape[0]
    features = activations.shape[1]
    width = enc_weight.shape[2]
    per_owner = tok_rows // groups
    block_of = block_ids[:, 0]
    matches = (block_of[:, None] == block_of[None, :]).astype(jnp.int32)
    earlier = jnp.sum(jnp.tril(matches, -1), axis=1)
    placed = block_of * per_owner + earlier
    source_row = (
        jnp.zeros((tok_rows,), jnp.int32).at[placed].set(jnp.arange(tok_rows, dtype=jnp.int32))
    )
    outgoing = activations[source_row.reshape(groups, per_owner)]
    rows_block = tok_rows * replicas
    incoming = lax.all_to_all(outgoing, "latent", split_axis=0, concat_axis=0, tiled=True)
    codes, grad_rows = fused_step(
        incoming, dec_bias, enc_weight[0], enc_bias, dec_weight[0], replicas=replicas
    )
    gathered = lax.all_to_all(grad_rows, "blk", split_axis=0, concat_axis=0, tiled=True)
    summed = jnp.sum(gathered[:, :width, :].astype(F32), axis=0)
    blk_pieces = gathered[:, width, :3].reshape(1, 1, replicas * 3)
    loss_row = jnp.pad(blk_pieces, ((0, 0), (0, 0), (0, width - replicas * 3)))
    loss_row = jnp.broadcast_to(loss_row, (groups, 1, width))
    sendback = jnp.concatenate([codes.transpose(1, 0, 2), loss_row], axis=1)
    returned = lax.all_to_all(sendback, "latent", split_axis=0, concat_axis=0, tiled=True)
    token_codes = returned[:, :per_owner, :].reshape(tok_rows, width)[placed]
    summed_loss = jnp.sum(returned[:, per_owner, :].astype(F32))
    gradient = summed / rows_block
    loss_value = summed_loss / (tok_rows * groups * replicas * features)
    return (loss_value, token_codes, gradient[None])


def solution(mesh):
    placed = (
        P(("latent", "blk"), None),
        P(("latent", "blk"), None),
        P("latent", None, None),
        P("latent", None),
        P("latent", None, None),
        P(),
    )
    return jax.shard_map(
        local,
        mesh=mesh,
        in_specs=placed,
        out_specs=(P(), P(("latent", "blk"), None), P("latent", None, "blk")),
        check_vma=False,
    )
```

```python
import functools
import jax
import jax.numpy as jnp
from jax import lax
from jax.experimental import pallas as pl
from jax.experimental.pallas import tpu as pltpu
from jax.sharding import PartitionSpec as P

F32 = jnp.float32
BF16 = jnp.bfloat16


def _pieces_row(s, lanes):
    hi = s.astype(BF16).astype(F32)
    mid = (s - hi).astype(BF16).astype(F32)
    lo = s - hi - mid
    lane = lax.broadcasted_iota(jnp.int32, (1, lanes), 1)
    row = jnp.where(lane == 0, hi, jnp.where(lane == 1, mid, jnp.where(lane == 2, lo, 0.0)))
    return row.astype(BF16)


def _sae_kernel(x_ref, bias_ref, enc_ref, encb_ref, dec_ref, codes_ref, grad_ref,
                acc_s, codes_s, codes_t_s, sq_s, *, n_tiles, tile, chunk, replicas):
    p = pl.program_id(0)
    t = pl.program_id(1)

    @pl.when((p == 0) & (t == 0))
    def _():
        acc_s[...] = jnp.zeros_like(acc_s)
        sq_s[...] = jnp.zeros_like(sq_s)

    @pl.when(p == 0)
    def _():
        for h in range(2):
            centered = (x_ref[:, h, :].astype(F32) - bias_ref[...]).astype(BF16)
            acc_s[h] += jnp.dot(centered, enc_ref[...], preferred_element_type=F32)

    @pl.when((p == 1) & (t == 0))
    def _():
        for h in range(2):
            codes = jnp.maximum(acc_s[h] + encb_ref[...], 0.0)
            codes_s[h] = codes.astype(BF16)
            codes_t_s[h] = codes.T.astype(BF16)
            codes_ref[h] = codes.astype(BF16)

    @pl.when(p == 1)
    def _():
        g = None
        for h in range(2):
            err = (jnp.dot(codes_s[h], dec_ref[...], preferred_element_type=F32)
                   + bias_ref[...] - x_ref[:, h, :].astype(F32))
            sq_s[...] += err * err
            part = jnp.dot(codes_t_s[h], err.astype(BF16), preferred_element_type=F32)
            g = part if g is None else g + part
        per = tile // chunk
        for q in range(per):
            grad_ref[t * per + q, 0:g.shape[0], :] = g[:, q * chunk:(q + 1) * chunk].astype(BF16)

    @pl.when((p == 1) & (t == n_tiles - 1))
    def _():
        col = jnp.sum(sq_s[...], axis=0, keepdims=True)
        s = jnp.sum(col, axis=1, keepdims=True)
        row = _pieces_row(s, chunk)
        width = codes_s.shape[2]
        for q in range(replicas):
            grad_ref[q, width:width + 1, :] = row


def _route_kernel(sel_ref, act_ref, out_ref):
    for h in range(out_ref.shape[1]):
        out_ref[:, h, :] = jnp.dot(
            sel_ref[h], act_ref[...], preferred_element_type=F32).astype(out_ref.dtype)


def route_rows(activations, placed, groups, tile=2048):
    rows, feat = activations.shape
    per = rows // groups
    slot = jnp.arange(rows, dtype=jnp.int32)
    sel = (placed[None, :] == slot[:, None]).astype(activations.dtype)
    sel = sel.reshape(groups, per, rows).transpose(1, 0, 2)
    return pl.pallas_call(
        _route_kernel,
        grid=(feat // tile,),
        in_specs=[
            pl.BlockSpec((per, groups, rows), lambda t: (0, 0, 0)),
            pl.BlockSpec((rows, tile), lambda t: (0, t)),
        ],
        out_specs=pl.BlockSpec((groups, per, tile), lambda t: (0, 0, t)),
        out_shape=jax.ShapeDtypeStruct((groups, per, feat), activations.dtype),
    )(sel, activations)


def fused_step(x, bias, enc, encb, dec, *, replicas, tile=2048, interpret=False):
    groups, _, feat = x.shape
    width = enc.shape[1]
    n_tiles = feat // tile
    chunk = feat // replicas
    kernel = functools.partial(_sae_kernel, n_tiles=n_tiles, tile=tile, chunk=chunk, replicas=replicas)

    def enc_map(p, t):
        return (t * (1 - p) + (n_tiles - 1) * p, 0)

    def dec_map(p, t):
        return (0, t * p)

    return pl.pallas_call(
        kernel,
        grid=(2, n_tiles),
        in_specs=[
            pl.BlockSpec((groups, 2, tile), lambda p, t: (0, 0, t)),
            pl.BlockSpec((1, tile), lambda p, t: (0, t)),
            pl.BlockSpec((tile, width), enc_map),
            pl.BlockSpec((1, width), lambda p, t: (0, 0)),
            pl.BlockSpec((width, tile), dec_map),
        ],
        out_specs=[
            pl.BlockSpec((2, groups, width), lambda p, t: (0, 0, 0)),
            pl.BlockSpec((replicas, width + 1, chunk), lambda p, t: (0, 0, 0)),
        ],
        out_shape=[
            jax.ShapeDtypeStruct((2, groups, width), BF16),
            jax.ShapeDtypeStruct((replicas, width + 1, chunk), BF16),
        ],
        scratch_shapes=[
            pltpu.VMEM((2, groups, width), F32),
            pltpu.VMEM((2, groups, width), BF16),
            pltpu.VMEM((2, width, groups), BF16),
            pltpu.VMEM((groups, tile), F32),
        ],
        compiler_params=pltpu.CompilerParams(
            dimension_semantics=("arbitrary", "arbitrary"),
            vmem_limit_bytes=48 * 1024 * 1024,
        ),
        interpret=interpret,
    )(x, bias.reshape(1, feat), enc, encb, dec)


def local(activations, block_ids, enc_weight, enc_bias, dec_weight, dec_bias):
    groups = lax.axis_size("latent")
    replicas = lax.axis_size("blk")
    tok_rows = activations.shape[0]
    features = activations.shape[1]
    width = enc_weight.shape[2]
    per_owner = tok_rows // groups
    block_of = block_ids[:, 0]
    matches = (block_of[:, None] == block_of[None, :]).astype(jnp.int32)
    earlier = jnp.sum(jnp.tril(matches, -1), axis=1)
    placed = block_of * per_owner + earlier
    outgoing = route_rows(activations, placed, groups)
    rows_block = tok_rows * replicas
    incoming = lax.all_to_all(outgoing, "latent", split_axis=0, concat_axis=0, tiled=True)
    codes, grad_rows = fused_step(
        incoming, dec_bias, enc_weight[0], enc_bias, dec_weight[0], replicas=replicas
    )
    gathered = lax.all_to_all(grad_rows, "blk", split_axis=0, concat_axis=0, tiled=True)
    summed = jnp.sum(gathered[:, :width, :].astype(F32), axis=0)
    blk_pieces = gathered[:, width, :3].reshape(1, 1, replicas * 3)
    loss_row = jnp.pad(blk_pieces, ((0, 0), (0, 0), (0, width - replicas * 3)))
    loss_row = jnp.broadcast_to(loss_row, (groups, 1, width))
    sendback = jnp.concatenate([codes.transpose(1, 0, 2), loss_row], axis=1)
    returned = lax.all_to_all(sendback, "latent", split_axis=0, concat_axis=0, tiled=True)
    token_codes = returned[:, :per_owner, :].reshape(tok_rows, width)[placed]
    summed_loss = jnp.sum(returned[:, per_owner, :].astype(F32))
    gradient = summed / rows_block
    loss_value = summed_loss / (tok_rows * groups * replicas * features)
    return (loss_value, token_codes, gradient[None])


def solution(mesh):
    placed = (
        P(("latent", "blk"), None),
        P(("latent", "blk"), None),
        P("latent", None, None),
        P("latent", None),
        P("latent", None, None),
        P(),
    )
    return jax.shard_map(
        local,
        mesh=mesh,
        in_specs=placed,
        out_specs=(P(), P(("latent", "blk"), None), P("latent", None, "blk")),
        check_vma=False,
    )
```

```python
import functools
import jax
import jax.numpy as jnp
from jax import lax
from jax.experimental import pallas as pl
from jax.experimental.pallas import tpu as pltpu
from jax.sharding import PartitionSpec as P

F32 = jnp.float32
BF16 = jnp.bfloat16


def _pieces_row(s, lanes):
    hi = s.astype(BF16).astype(F32)
    mid = (s - hi).astype(BF16).astype(F32)
    lo = s - hi - mid
    lane = lax.broadcasted_iota(jnp.int32, (1, lanes), 1)
    row = jnp.where(lane == 0, hi, jnp.where(lane == 1, mid, jnp.where(lane == 2, lo, 0.0)))
    return row.astype(BF16)


def _sae_kernel(x_ref, bias_ref, enc_ref, encb_ref, dec_ref, codes_ref, grad_ref,
                acc_s, codes_s, codes_t_s, sq_s, *, n_tiles, tile, chunk, replicas):
    p = pl.program_id(0)
    t = pl.program_id(1)

    @pl.when((p == 0) & (t == 0))
    def _():
        acc_s[...] = jnp.zeros_like(acc_s)
        sq_s[...] = jnp.zeros_like(sq_s)

    @pl.when(p == 0)
    def _():
        for h in range(2):
            centered = (x_ref[:, h, :].astype(F32) - bias_ref[...]).astype(BF16)
            acc_s[h] += jnp.dot(centered, enc_ref[...], preferred_element_type=F32)

    @pl.when((p == 1) & (t == 0))
    def _():
        for h in range(2):
            codes = jnp.maximum(acc_s[h] + encb_ref[...], 0.0)
            codes_s[h] = codes.astype(BF16)
            codes_t_s[h] = codes.T.astype(BF16)
            codes_ref[h] = codes.astype(BF16)

    @pl.when(p == 1)
    def _():
        g = None
        for h in range(2):
            err = (jnp.dot(codes_s[h], dec_ref[...], preferred_element_type=F32)
                   + bias_ref[...] - x_ref[:, h, :].astype(F32))
            sq_s[...] += err * err
            part = jnp.dot(codes_t_s[h], err.astype(BF16), preferred_element_type=F32)
            g = part if g is None else g + part
        per = tile // chunk
        for q in range(per):
            grad_ref[t * per + q, 0:g.shape[0], :] = g[:, q * chunk:(q + 1) * chunk].astype(BF16)

    @pl.when((p == 1) & (t == n_tiles - 1))
    def _():
        col = jnp.sum(sq_s[...], axis=0, keepdims=True)
        s = jnp.sum(col, axis=1, keepdims=True)
        row = _pieces_row(s, chunk)
        width = codes_s.shape[2]
        for q in range(replicas):
            grad_ref[q, width:width + 1, :] = row


def _route_kernel(col_ref, row_ref, act_ref, out_ref):
    groups, per, _ = out_ref.shape
    rows = col_ref.shape[0]
    same = col_ref[...] == row_ref[...]
    before = (lax.broadcasted_iota(jnp.int32, (rows, rows), 0)
              < lax.broadcasted_iota(jnp.int32, (rows, rows), 1))
    earlier = jnp.sum(jnp.where(same & before, 1.0, 0.0), axis=0, keepdims=True)
    placed = row_ref[...].astype(F32) * per + earlier
    slot = lax.broadcasted_iota(jnp.int32, (groups, rows), 0).astype(F32) * per
    for h in range(per):
        sel = jnp.where(placed == slot + h, 1.0, 0.0).astype(act_ref.dtype)
        out_ref[:, h, :] = jnp.dot(
            sel, act_ref[...], preferred_element_type=F32).astype(out_ref.dtype)


def route_rows(activations, block_ids, groups, tile=2048):
    rows, feat = activations.shape
    per = rows // groups
    return pl.pallas_call(
        _route_kernel,
        grid=(feat // tile,),
        in_specs=[
            pl.BlockSpec((rows, 1), lambda t: (0, 0)),
            pl.BlockSpec((1, rows), lambda t: (0, 0)),
            pl.BlockSpec((rows, tile), lambda t: (0, t)),
        ],
        out_specs=pl.BlockSpec((groups, per, tile), lambda t: (0, 0, t)),
        out_shape=jax.ShapeDtypeStruct((groups, per, feat), activations.dtype),
    )(block_ids, block_ids.reshape(1, rows), activations)


def fused_step(x, bias, enc, encb, dec, *, replicas, tile=2048, interpret=False):
    groups, _, feat = x.shape
    width = enc.shape[1]
    n_tiles = feat // tile
    chunk = feat // replicas
    kernel = functools.partial(_sae_kernel, n_tiles=n_tiles, tile=tile, chunk=chunk, replicas=replicas)

    def enc_map(p, t):
        return (t * (1 - p) + (n_tiles - 1) * p, 0)

    def dec_map(p, t):
        return (0, t * p)

    return pl.pallas_call(
        kernel,
        grid=(2, n_tiles),
        in_specs=[
            pl.BlockSpec((groups, 2, tile), lambda p, t: (0, 0, t)),
            pl.BlockSpec((1, tile), lambda p, t: (0, t)),
            pl.BlockSpec((tile, width), enc_map),
            pl.BlockSpec((1, width), lambda p, t: (0, 0)),
            pl.BlockSpec((width, tile), dec_map),
        ],
        out_specs=[
            pl.BlockSpec((2, groups, width), lambda p, t: (0, 0, 0)),
            pl.BlockSpec((replicas, width + 1, chunk), lambda p, t: (0, 0, 0)),
        ],
        out_shape=[
            jax.ShapeDtypeStruct((2, groups, width), BF16),
            jax.ShapeDtypeStruct((replicas, width + 1, chunk), BF16),
        ],
        scratch_shapes=[
            pltpu.VMEM((2, groups, width), F32),
            pltpu.VMEM((2, groups, width), BF16),
            pltpu.VMEM((2, width, groups), BF16),
            pltpu.VMEM((groups, tile), F32),
        ],
        compiler_params=pltpu.CompilerParams(
            dimension_semantics=("arbitrary", "arbitrary"),
            vmem_limit_bytes=48 * 1024 * 1024,
        ),
        interpret=interpret,
    )(x, bias.reshape(1, feat), enc, encb, dec)


def local(activations, block_ids, enc_weight, enc_bias, dec_weight, dec_bias):
    groups = lax.axis_size("latent")
    replicas = lax.axis_size("blk")
    tok_rows = activations.shape[0]
    features = activations.shape[1]
    width = enc_weight.shape[2]
    per_owner = tok_rows // groups
    block_of = block_ids[:, 0]
    matches = (block_of[:, None] == block_of[None, :]).astype(jnp.int32)
    earlier = jnp.sum(jnp.tril(matches, -1), axis=1)
    placed = block_of * per_owner + earlier
    outgoing = route_rows(activations, block_ids, groups)
    rows_block = tok_rows * replicas
    incoming = lax.all_to_all(outgoing, "latent", split_axis=0, concat_axis=0, tiled=True)
    codes, grad_rows = fused_step(
        incoming, dec_bias, enc_weight[0], enc_bias, dec_weight[0], replicas=replicas
    )
    gathered = lax.all_to_all(grad_rows, "blk", split_axis=0, concat_axis=0, tiled=True)
    summed = jnp.sum(gathered[:, :width, :].astype(F32), axis=0)
    blk_pieces = gathered[:, width, :3].reshape(1, 1, replicas * 3)
    loss_row = jnp.pad(blk_pieces, ((0, 0), (0, 0), (0, width - replicas * 3)))
    loss_row = jnp.broadcast_to(loss_row, (groups, 1, width))
    sendback = jnp.concatenate([codes.transpose(1, 0, 2), loss_row], axis=1)
    returned = lax.all_to_all(sendback, "latent", split_axis=0, concat_axis=0, tiled=True)
    token_codes = returned[:, :per_owner, :].reshape(tok_rows, width)[placed]
    summed_loss = jnp.sum(returned[:, per_owner, :].astype(F32))
    gradient = summed / rows_block
    loss_value = summed_loss / (tok_rows * groups * replicas * features)
    return (loss_value, token_codes, gradient[None])


def solution(mesh):
    placed = (
        P(("latent", "blk"), None),
        P(("latent", "blk"), None),
        P("latent", None, None),
        P("latent", None),
        P("latent", None, None),
        P(),
    )
    return jax.shard_map(
        local,
        mesh=mesh,
        in_specs=placed,
        out_specs=(P(), P(("latent", "blk"), None), P("latent", None, "blk")),
        check_vma=False,
    )
```

```python
import functools
import jax
import jax.numpy as jnp
from jax import lax
from jax.experimental import pallas as pl
from jax.experimental.pallas import tpu as pltpu
from jax.sharding import PartitionSpec as P

F32 = jnp.float32
BF16 = jnp.bfloat16


def _pieces_row(s, lanes):
    hi = s.astype(BF16).astype(F32)
    mid = (s - hi).astype(BF16).astype(F32)
    lo = s - hi - mid
    lane = lax.broadcasted_iota(jnp.int32, (1, lanes), 1)
    row = jnp.where(lane == 0, hi, jnp.where(lane == 1, mid, jnp.where(lane == 2, lo, 0.0)))
    return row.astype(BF16)


def _sae_kernel(x_ref, bias_ref, enc_ref, encb_ref, dec_ref, codes_ref, grad_ref,
                acc_s, codes_s, codes_t_s, sq_s, *, n_tiles, tile, chunk, replicas):
    p = pl.program_id(0)
    t = pl.program_id(1)

    @pl.when((p == 0) & (t == 0))
    def _():
        acc_s[...] = jnp.zeros_like(acc_s)
        sq_s[...] = jnp.zeros_like(sq_s)

    @pl.when(p == 0)
    def _():
        x = jnp.concatenate([x_ref[:, 0, :], x_ref[:, 1, :]], axis=0).astype(F32)
        centered = (x - bias_ref[...]).astype(BF16)
        acc_s[...] += jnp.dot(centered, enc_ref[...], preferred_element_type=F32)

    @pl.when((p == 1) & (t == 0))
    def _():
        codes = jnp.maximum(acc_s[...] + encb_ref[...], 0.0)
        codes_s[...] = codes.astype(BF16)
        codes_t_s[...] = codes.T.astype(BF16)
        half = codes.shape[0] // 2
        for h in range(2):
            codes_ref[h] = codes[h * half:(h + 1) * half].astype(BF16)

    @pl.when(p == 1)
    def _():
        x = jnp.concatenate([x_ref[:, 0, :], x_ref[:, 1, :]], axis=0).astype(F32)
        err = (jnp.dot(codes_s[...], dec_ref[...], preferred_element_type=F32)
               + bias_ref[...] - x)
        sq_s[...] += err * err
        g = jnp.dot(codes_t_s[...], err.astype(BF16), preferred_element_type=F32)
        per = tile // chunk
        for q in range(per):
            grad_ref[t * per + q, 0:g.shape[0], :] = g[:, q * chunk:(q + 1) * chunk].astype(BF16)

    @pl.when((p == 1) & (t == n_tiles - 1))
    def _():
        col = jnp.sum(sq_s[...], axis=0, keepdims=True)
        s = jnp.sum(col, axis=1, keepdims=True)
        row = _pieces_row(s, chunk)
        width = codes_s.shape[1]
        for q in range(replicas):
            grad_ref[q, width:width + 1, :] = row


def _route_kernel(col_ref, row_ref, act_ref, out_ref):
    groups, per, _ = out_ref.shape
    rows = col_ref.shape[0]
    same = col_ref[...] == row_ref[...]
    before = (lax.broadcasted_iota(jnp.int32, (rows, rows), 0)
              < lax.broadcasted_iota(jnp.int32, (rows, rows), 1))
    earlier = jnp.sum(jnp.where(same & before, 1.0, 0.0), axis=0, keepdims=True)
    placed = row_ref[...].astype(F32) * per + earlier
    slot = lax.broadcasted_iota(jnp.int32, (groups, rows), 0).astype(F32) * per
    for h in range(per):
        sel = jnp.where(placed == slot + h, 1.0, 0.0).astype(act_ref.dtype)
        out_ref[:, h, :] = jnp.dot(
            sel, act_ref[...], preferred_element_type=F32).astype(out_ref.dtype)


def route_rows(activations, block_ids, groups, tile=4096):
    rows, feat = activations.shape
    per = rows // groups
    return pl.pallas_call(
        _route_kernel,
        grid=(feat // tile,),
        in_specs=[
            pl.BlockSpec((rows, 1), lambda t: (0, 0)),
            pl.BlockSpec((1, rows), lambda t: (0, 0)),
            pl.BlockSpec((rows, tile), lambda t: (0, t)),
        ],
        out_specs=pl.BlockSpec((groups, per, tile), lambda t: (0, 0, t)),
        out_shape=jax.ShapeDtypeStruct((groups, per, feat), activations.dtype),
    )(block_ids, block_ids.reshape(1, rows), activations)


def fused_step(x, bias, enc, encb, dec, *, replicas, tile=4096, interpret=False):
    groups, _, feat = x.shape
    width = enc.shape[1]
    n_tiles = feat // tile
    chunk = feat // replicas
    kernel = functools.partial(_sae_kernel, n_tiles=n_tiles, tile=tile, chunk=chunk, replicas=replicas)

    def enc_map(p, t):
        return (t * (1 - p) + (n_tiles - 1) * p, 0)

    def dec_map(p, t):
        return (0, t * p)

    return pl.pallas_call(
        kernel,
        grid=(2, n_tiles),
        in_specs=[
            pl.BlockSpec((groups, 2, tile), lambda p, t: (0, 0, t)),
            pl.BlockSpec((1, tile), lambda p, t: (0, t)),
            pl.BlockSpec((tile, width), enc_map),
            pl.BlockSpec((1, width), lambda p, t: (0, 0)),
            pl.BlockSpec((width, tile), dec_map),
        ],
        out_specs=[
            pl.BlockSpec((2, groups, width), lambda p, t: (0, 0, 0)),
            pl.BlockSpec((replicas, width + 1, chunk), lambda p, t: (0, 0, 0)),
        ],
        out_shape=[
            jax.ShapeDtypeStruct((2, groups, width), BF16),
            jax.ShapeDtypeStruct((replicas, width + 1, chunk), BF16),
        ],
        scratch_shapes=[
            pltpu.VMEM((2 * groups, width), F32),
            pltpu.VMEM((2 * groups, width), BF16),
            pltpu.VMEM((width, 2 * groups), BF16),
            pltpu.VMEM((2 * groups, tile), F32),
        ],
        compiler_params=pltpu.CompilerParams(
            dimension_semantics=("arbitrary", "arbitrary"),
            vmem_limit_bytes=48 * 1024 * 1024,
        ),
        interpret=interpret,
    )(x, bias.reshape(1, feat), enc, encb, dec)


def local(activations, block_ids, enc_weight, enc_bias, dec_weight, dec_bias):
    groups = lax.axis_size("latent")
    replicas = lax.axis_size("blk")
    tok_rows = activations.shape[0]
    features = activations.shape[1]
    width = enc_weight.shape[2]
    per_owner = tok_rows // groups
    block_of = block_ids[:, 0]
    matches = (block_of[:, None] == block_of[None, :]).astype(jnp.int32)
    earlier = jnp.sum(jnp.tril(matches, -1), axis=1)
    placed = block_of * per_owner + earlier
    outgoing = route_rows(activations, block_ids, groups)
    rows_block = tok_rows * replicas
    incoming = lax.all_to_all(outgoing, "latent", split_axis=0, concat_axis=0, tiled=True)
    codes, grad_rows = fused_step(
        incoming, dec_bias, enc_weight[0], enc_bias, dec_weight[0], replicas=replicas
    )
    gathered = lax.all_to_all(grad_rows, "blk", split_axis=0, concat_axis=0, tiled=True)
    summed = jnp.sum(gathered[:, :width, :].astype(F32), axis=0)
    blk_pieces = gathered[:, width, :3].reshape(1, 1, replicas * 3)
    loss_row = jnp.pad(blk_pieces, ((0, 0), (0, 0), (0, width - replicas * 3)))
    loss_row = jnp.broadcast_to(loss_row, (groups, 1, width))
    sendback = jnp.concatenate([codes.transpose(1, 0, 2), loss_row], axis=1)
    returned = lax.all_to_all(sendback, "latent", split_axis=0, concat_axis=0, tiled=True)
    token_codes = returned[:, :per_owner, :].reshape(tok_rows, width)[placed]
    summed_loss = jnp.sum(returned[:, per_owner, :].astype(F32))
    gradient = summed / rows_block
    loss_value = summed_loss / (tok_rows * groups * replicas * features)
    return (loss_value, token_codes, gradient[None])


def solution(mesh):
    placed = (
        P(("latent", "blk"), None),
        P(("latent", "blk"), None),
        P("latent", None, None),
        P("latent", None),
        P("latent", None, None),
        P(),
    )
    return jax.shard_map(
        local,
        mesh=mesh,
        in_specs=placed,
        out_specs=(P(), P(("latent", "blk"), None), P("latent", None, "blk")),
        check_vma=False,
    )
```

```python
import functools
import jax
import jax.numpy as jnp
from jax import lax
from jax.experimental import pallas as pl
from jax.experimental.pallas import tpu as pltpu
from jax.sharding import PartitionSpec as P

F32 = jnp.float32
BF16 = jnp.bfloat16


def _pieces_row(s, lanes):
    hi = s.astype(BF16).astype(F32)
    mid = (s - hi).astype(BF16).astype(F32)
    lo = s - hi - mid
    lane = lax.broadcasted_iota(jnp.int32, (1, lanes), 1)
    row = jnp.where(lane == 0, hi, jnp.where(lane == 1, mid, jnp.where(lane == 2, lo, 0.0)))
    return row.astype(BF16)


def _sae_kernel(x_ref, bias_ref, enc_ref, encb_ref, dec_ref, codes_ref, grad_ref,
                acc_s, codes_s, codes_t_s, sq_s, *, n_tiles, tile, chunk, replicas):
    p = pl.program_id(0)
    t = pl.program_id(1)

    @pl.when((p == 0) & (t == 0))
    def _():
        acc_s[...] = jnp.zeros_like(acc_s)
        sq_s[...] = jnp.zeros_like(sq_s)

    @pl.when(p == 0)
    def _():
        for h in range(2):
            centered = (x_ref[:, h, :].astype(F32) - bias_ref[...]).astype(BF16)
            acc_s[h] += jnp.dot(centered, enc_ref[...], preferred_element_type=F32)

    @pl.when((p == 1) & (t == 0))
    def _():
        for h in range(2):
            codes = jnp.maximum(acc_s[h] + encb_ref[...], 0.0)
            codes_s[h] = codes.astype(BF16)
            codes_t_s[h] = codes.T.astype(BF16)
            codes_ref[h] = codes.astype(BF16)

    @pl.when(p == 1)
    def _():
        g = None
        for h in range(2):
            err = (jnp.dot(codes_s[h], dec_ref[...], preferred_element_type=F32)
                   + bias_ref[...] - x_ref[:, h, :].astype(F32))
            sq_s[...] += err * err
            part = jnp.dot(codes_t_s[h], err.astype(BF16), preferred_element_type=F32)
            g = part if g is None else g + part
        per = tile // chunk
        for q in range(per):
            grad_ref[t * per + q, 0:g.shape[0], :] = g[:, q * chunk:(q + 1) * chunk].astype(BF16)

    @pl.when((p == 1) & (t == n_tiles - 1))
    def _():
        col = jnp.sum(sq_s[...], axis=0, keepdims=True)
        s = jnp.sum(col, axis=1, keepdims=True)
        row = _pieces_row(s, chunk)
        width = codes_s.shape[2]
        for q in range(replicas):
            grad_ref[q, width:width + 1, :] = row


def _route_kernel(col_ref, row_ref, act_ref, out_ref):
    groups, per, _ = out_ref.shape
    rows = col_ref.shape[0]
    same = col_ref[...] == row_ref[...]
    before = (lax.broadcasted_iota(jnp.int32, (rows, rows), 0)
              < lax.broadcasted_iota(jnp.int32, (rows, rows), 1))
    earlier = jnp.sum(jnp.where(same & before, 1.0, 0.0), axis=0, keepdims=True)
    placed = row_ref[...].astype(F32) * per + earlier
    slot = lax.broadcasted_iota(jnp.int32, (groups, rows), 0).astype(F32) * per
    for h in range(per):
        sel = jnp.where(placed == slot + h, 1.0, 0.0).astype(act_ref.dtype)
        out_ref[:, h, :] = jnp.dot(
            sel, act_ref[...], preferred_element_type=F32).astype(out_ref.dtype)


def route_rows(activations, block_ids, groups, tile=4096):
    rows, feat = activations.shape
    per = rows // groups
    return pl.pallas_call(
        _route_kernel,
        grid=(feat // tile,),
        in_specs=[
            pl.BlockSpec((rows, 1), lambda t: (0, 0)),
            pl.BlockSpec((1, rows), lambda t: (0, 0)),
            pl.BlockSpec((rows, tile), lambda t: (0, t)),
        ],
        out_specs=pl.BlockSpec((groups, per, tile), lambda t: (0, 0, t)),
        out_shape=jax.ShapeDtypeStruct((groups, per, feat), activations.dtype),
    )(block_ids, block_ids.reshape(1, rows), activations)


def fused_step(x, bias, enc, encb, dec, *, replicas, tile=2048, interpret=False):
    groups, _, feat = x.shape
    width = enc.shape[1]
    n_tiles = feat // tile
    chunk = feat // replicas
    kernel = functools.partial(_sae_kernel, n_tiles=n_tiles, tile=tile, chunk=chunk, replicas=replicas)

    def enc_map(p, t):
        return (t * (1 - p) + (n_tiles - 1) * p, 0)

    def dec_map(p, t):
        return (0, t * p)

    return pl.pallas_call(
        kernel,
        grid=(2, n_tiles),
        in_specs=[
            pl.BlockSpec((groups, 2, tile), lambda p, t: (0, 0, t)),
            pl.BlockSpec((1, tile), lambda p, t: (0, t)),
            pl.BlockSpec((tile, width), enc_map),
            pl.BlockSpec((1, width), lambda p, t: (0, 0)),
            pl.BlockSpec((width, tile), dec_map),
        ],
        out_specs=[
            pl.BlockSpec((2, groups, width), lambda p, t: (0, 0, 0)),
            pl.BlockSpec((replicas, width + 1, chunk), lambda p, t: (0, 0, 0)),
        ],
        out_shape=[
            jax.ShapeDtypeStruct((2, groups, width), BF16),
            jax.ShapeDtypeStruct((replicas, width + 1, chunk), BF16),
        ],
        scratch_shapes=[
            pltpu.VMEM((2, groups, width), F32),
            pltpu.VMEM((2, groups, width), BF16),
            pltpu.VMEM((2, width, groups), BF16),
            pltpu.VMEM((groups, tile), F32),
        ],
        compiler_params=pltpu.CompilerParams(
            dimension_semantics=("arbitrary", "arbitrary"),
            vmem_limit_bytes=48 * 1024 * 1024,
        ),
        interpret=interpret,
    )(x, bias.reshape(1, feat), enc, encb, dec)


def local(activations, block_ids, enc_weight, enc_bias, dec_weight, dec_bias):
    groups = lax.axis_size("latent")
    replicas = lax.axis_size("blk")
    tok_rows = activations.shape[0]
    features = activations.shape[1]
    width = enc_weight.shape[2]
    per_owner = tok_rows // groups
    block_of = block_ids[:, 0]
    matches = (block_of[:, None] == block_of[None, :]).astype(jnp.int32)
    earlier = jnp.sum(jnp.tril(matches, -1), axis=1)
    placed = block_of * per_owner + earlier
    outgoing = route_rows(activations, block_ids, groups)
    rows_block = tok_rows * replicas
    incoming = lax.all_to_all(outgoing, "latent", split_axis=0, concat_axis=0, tiled=True)
    codes, grad_rows = fused_step(
        incoming, dec_bias, enc_weight[0], enc_bias, dec_weight[0], replicas=replicas
    )
    gathered = lax.all_to_all(grad_rows, "blk", split_axis=0, concat_axis=0, tiled=True)
    summed = jnp.sum(gathered[:, :width, :].astype(F32), axis=0)
    blk_pieces = gathered[:, width, :3].reshape(1, 1, replicas * 3)
    loss_row = jnp.pad(blk_pieces, ((0, 0), (0, 0), (0, width - replicas * 3)))
    loss_row = jnp.broadcast_to(loss_row, (groups, 1, width))
    sendback = jnp.concatenate([codes.transpose(1, 0, 2), loss_row], axis=1)
    returned = lax.all_to_all(sendback, "latent", split_axis=0, concat_axis=0, tiled=True)
    token_codes = returned[:, :per_owner, :].reshape(tok_rows, width)[placed]
    summed_loss = jnp.sum(returned[:, per_owner, :].astype(F32))
    gradient = summed / rows_block
    loss_value = summed_loss / (tok_rows * groups * replicas * features)
    return (loss_value, token_codes, gradient[None])


def solution(mesh):
    placed = (
        P(("latent", "blk"), None),
        P(("latent", "blk"), None),
        P("latent", None, None),
        P("latent", None),
        P("latent", None, None),
        P(),
    )
    return jax.shard_map(
        local,
        mesh=mesh,
        in_specs=placed,
        out_specs=(P(), P(("latent", "blk"), None), P("latent", None, "blk")),
        check_vma=False,
    )
```

```python
import functools
import jax
import jax.numpy as jnp
from jax import lax
from jax.experimental import pallas as pl
from jax.experimental.pallas import tpu as pltpu
from jax.sharding import PartitionSpec as P

F32 = jnp.float32
BF16 = jnp.bfloat16


def _pieces_row(s, lanes):
    hi = s.astype(BF16).astype(F32)
    mid = (s - hi).astype(BF16).astype(F32)
    lo = s - hi - mid
    lane = lax.broadcasted_iota(jnp.int32, (1, lanes), 1)
    row = jnp.where(lane == 0, hi, jnp.where(lane == 1, mid, jnp.where(lane == 2, lo, 0.0)))
    return row.astype(BF16)


def _sae_kernel(x_ref, bias_ref, enc_ref, encb_ref, dec_ref, codes_ref, grad_ref,
                acc_s, codes_s, codes_t_s, sq_s, *, n_tiles, tile, chunk, replicas):
    p = pl.program_id(0)
    t = pl.program_id(1)
    cols = pl.ds(pl.multiple_of(t * tile, tile), tile)

    @pl.when((p == 0) & (t == 0))
    def _():
        acc_s[...] = jnp.zeros_like(acc_s)
        sq_s[...] = jnp.zeros_like(sq_s)

    @pl.when(p == 0)
    def _():
        for h in range(2):
            centered = (x_ref[:, h, cols].astype(F32) - bias_ref[...]).astype(BF16)
            acc_s[h] += jnp.dot(centered, enc_ref[...], preferred_element_type=F32)

    @pl.when((p == 1) & (t == 0))
    def _():
        for h in range(2):
            codes = jnp.maximum(acc_s[h] + encb_ref[...], 0.0)
            codes_s[h] = codes.astype(BF16)
            codes_t_s[h] = codes.T.astype(BF16)
            codes_ref[h] = codes.astype(BF16)

    @pl.when(p == 1)
    def _():
        g = None
        for h in range(2):
            err = (jnp.dot(codes_s[h], dec_ref[...], preferred_element_type=F32)
                   + bias_ref[...] - x_ref[:, h, cols].astype(F32))
            sq_s[...] += err * err
            part = jnp.dot(codes_t_s[h], err.astype(BF16), preferred_element_type=F32)
            g = part if g is None else g + part
        per = tile // chunk
        for q in range(per):
            grad_ref[t * per + q, 0:g.shape[0], :] = g[:, q * chunk:(q + 1) * chunk].astype(BF16)

    @pl.when((p == 1) & (t == n_tiles - 1))
    def _():
        col = jnp.sum(sq_s[...], axis=0, keepdims=True)
        s = jnp.sum(col, axis=1, keepdims=True)
        row = _pieces_row(s, chunk)
        width = codes_s.shape[2]
        for q in range(replicas):
            grad_ref[q, width:width + 1, :] = row


def _route_kernel(col_ref, row_ref, act_ref, out_ref):
    groups, per, _ = out_ref.shape
    rows = col_ref.shape[0]
    same = col_ref[...] == row_ref[...]
    before = (lax.broadcasted_iota(jnp.int32, (rows, rows), 0)
              < lax.broadcasted_iota(jnp.int32, (rows, rows), 1))
    earlier = jnp.sum(jnp.where(same & before, 1.0, 0.0), axis=0, keepdims=True)
    placed = row_ref[...].astype(F32) * per + earlier
    slot = lax.broadcasted_iota(jnp.int32, (groups, rows), 0).astype(F32) * per
    for h in range(per):
        sel = jnp.where(placed == slot + h, 1.0, 0.0).astype(act_ref.dtype)
        out_ref[:, h, :] = jnp.dot(
            sel, act_ref[...], preferred_element_type=F32).astype(out_ref.dtype)


def route_rows(activations, block_ids, groups, tile=4096):
    rows, feat = activations.shape
    per = rows // groups
    return pl.pallas_call(
        _route_kernel,
        grid=(feat // tile,),
        in_specs=[
            pl.BlockSpec((rows, 1), lambda t: (0, 0)),
            pl.BlockSpec((1, rows), lambda t: (0, 0)),
            pl.BlockSpec((rows, tile), lambda t: (0, t)),
        ],
        out_specs=pl.BlockSpec((groups, per, tile), lambda t: (0, 0, t)),
        out_shape=jax.ShapeDtypeStruct((groups, per, feat), activations.dtype),
    )(block_ids, block_ids.reshape(1, rows), activations)


def fused_step(x, bias, enc, encb, dec, *, replicas, tile=2048, interpret=False):
    groups, _, feat = x.shape
    width = enc.shape[1]
    n_tiles = feat // tile
    chunk = feat // replicas
    kernel = functools.partial(_sae_kernel, n_tiles=n_tiles, tile=tile, chunk=chunk, replicas=replicas)

    def enc_map(p, t):
        return (t * (1 - p) + (n_tiles - 1) * p, 0)

    def dec_map(p, t):
        return (0, t * p)

    return pl.pallas_call(
        kernel,
        grid=(2, n_tiles),
        in_specs=[
            pl.BlockSpec(memory_space=pltpu.VMEM),
            pl.BlockSpec((1, tile), lambda p, t: (0, t)),
            pl.BlockSpec((tile, width), enc_map),
            pl.BlockSpec((1, width), lambda p, t: (0, 0)),
            pl.BlockSpec((width, tile), dec_map),
        ],
        out_specs=[
            pl.BlockSpec((2, groups, width), lambda p, t: (0, 0, 0)),
            pl.BlockSpec((replicas, width + 1, chunk), lambda p, t: (0, 0, 0)),
        ],
        out_shape=[
            jax.ShapeDtypeStruct((2, groups, width), BF16),
            jax.ShapeDtypeStruct((replicas, width + 1, chunk), BF16),
        ],
        scratch_shapes=[
            pltpu.VMEM((2, groups, width), F32),
            pltpu.VMEM((2, groups, width), BF16),
            pltpu.VMEM((2, width, groups), BF16),
            pltpu.VMEM((groups, tile), F32),
        ],
        compiler_params=pltpu.CompilerParams(
            dimension_semantics=("arbitrary", "arbitrary"),
            vmem_limit_bytes=48 * 1024 * 1024,
        ),
        interpret=interpret,
    )(x, bias.reshape(1, feat), enc, encb, dec)


def local(activations, block_ids, enc_weight, enc_bias, dec_weight, dec_bias):
    groups = lax.axis_size("latent")
    replicas = lax.axis_size("blk")
    tok_rows = activations.shape[0]
    features = activations.shape[1]
    width = enc_weight.shape[2]
    per_owner = tok_rows // groups
    block_of = block_ids[:, 0]
    matches = (block_of[:, None] == block_of[None, :]).astype(jnp.int32)
    earlier = jnp.sum(jnp.tril(matches, -1), axis=1)
    placed = block_of * per_owner + earlier
    outgoing = route_rows(activations, block_ids, groups)
    rows_block = tok_rows * replicas
    incoming = lax.all_to_all(outgoing, "latent", split_axis=0, concat_axis=0, tiled=True)
    codes, grad_rows = fused_step(
        incoming, dec_bias, enc_weight[0], enc_bias, dec_weight[0], replicas=replicas
    )
    gathered = lax.all_to_all(grad_rows, "blk", split_axis=0, concat_axis=0, tiled=True)
    summed = jnp.sum(gathered[:, :width, :].astype(F32), axis=0)
    blk_pieces = gathered[:, width, :3].reshape(1, 1, replicas * 3)
    loss_row = jnp.pad(blk_pieces, ((0, 0), (0, 0), (0, width - replicas * 3)))
    loss_row = jnp.broadcast_to(loss_row, (groups, 1, width))
    sendback = jnp.concatenate([codes.transpose(1, 0, 2), loss_row], axis=1)
    returned = lax.all_to_all(sendback, "latent", split_axis=0, concat_axis=0, tiled=True)
    token_codes = returned[:, :per_owner, :].reshape(tok_rows, width)[placed]
    summed_loss = jnp.sum(returned[:, per_owner, :].astype(F32))
    gradient = summed / rows_block
    loss_value = summed_loss / (tok_rows * groups * replicas * features)
    return (loss_value, token_codes, gradient[None])


def solution(mesh):
    placed = (
        P(("latent", "blk"), None),
        P(("latent", "blk"), None),
        P("latent", None, None),
        P("latent", None),
        P("latent", None, None),
        P(),
    )
    return jax.shard_map(
        local,
        mesh=mesh,
        in_specs=placed,
        out_specs=(P(), P(("latent", "blk"), None), P("latent", None, "blk")),
        check_vma=False,
    )
```

```python
import functools
import jax
import jax.numpy as jnp
from jax import lax
from jax.experimental import pallas as pl
from jax.experimental.pallas import tpu as pltpu
from jax.sharding import PartitionSpec as P

F32 = jnp.float32
BF16 = jnp.bfloat16


def _pieces_row(s, lanes):
    hi = s.astype(BF16).astype(F32)
    mid = (s - hi).astype(BF16).astype(F32)
    lo = s - hi - mid
    lane = lax.broadcasted_iota(jnp.int32, (1, lanes), 1)
    row = jnp.where(lane == 0, hi, jnp.where(lane == 1, mid, jnp.where(lane == 2, lo, 0.0)))
    return row.astype(BF16)


def _sae_kernel(x_ref, bias_ref, enc_ref, encb_ref, dec_ref, codes_ref, grad_ref,
                acc_s, codes_s, codes_t_s, sq_s, *, n_tiles, tile, chunk, replicas):
    p = pl.program_id(0)
    t = pl.program_id(1)
    cols = pl.ds(pl.multiple_of(t * tile, tile), tile)

    @pl.when((p == 0) & (t == 0))
    def _():
        acc_s[...] = jnp.zeros_like(acc_s)
        sq_s[...] = jnp.zeros_like(sq_s)

    @pl.when(p == 0)
    def _():
        for h in range(2):
            centered = (x_ref[:, h, cols].astype(F32) - bias_ref[...]).astype(BF16)
            acc_s[h] += jnp.dot(centered, enc_ref[...], preferred_element_type=F32)

    @pl.when((p == 1) & (t == 0))
    def _():
        for h in range(2):
            codes = jnp.maximum(acc_s[h] + encb_ref[...], 0.0)
            codes_s[h] = codes.astype(BF16)
            codes_t_s[h] = codes.T.astype(BF16)
            codes_ref[h] = codes.astype(BF16)

    @pl.when(p == 1)
    def _():
        g = None
        for h in range(2):
            err = (jnp.dot(codes_s[h], dec_ref[...], preferred_element_type=F32)
                   + bias_ref[...] - x_ref[:, h, cols].astype(F32))
            sq_s[...] += err * err
            part = jnp.dot(codes_t_s[h], err.astype(BF16), preferred_element_type=F32)
            g = part if g is None else g + part
        per = tile // chunk
        for q in range(per):
            grad_ref[t * per + q, 0:g.shape[0], :] = g[:, q * chunk:(q + 1) * chunk].astype(BF16)

    @pl.when((p == 1) & (t == n_tiles - 1))
    def _():
        col = jnp.sum(sq_s[...], axis=0, keepdims=True)
        s = jnp.sum(col, axis=1, keepdims=True)
        row = _pieces_row(s, chunk)
        width = codes_s.shape[2]
        for q in range(replicas):
            grad_ref[q, width:width + 1, :] = row


def _route_kernel(col_ref, row_ref, act_ref, out_ref):
    groups, per, _ = out_ref.shape
    rows = col_ref.shape[0]
    same = col_ref[...] == row_ref[...]
    before = (lax.broadcasted_iota(jnp.int32, (rows, rows), 0)
              < lax.broadcasted_iota(jnp.int32, (rows, rows), 1))
    earlier = jnp.sum(jnp.where(same & before, 1.0, 0.0), axis=0, keepdims=True)
    placed = row_ref[...].astype(F32) * per + earlier
    slot = lax.broadcasted_iota(jnp.int32, (groups, rows), 0).astype(F32) * per
    for h in range(per):
        sel = jnp.where(placed == slot + h, 1.0, 0.0).astype(act_ref.dtype)
        out_ref[:, h, :] = jnp.dot(
            sel, act_ref[...], preferred_element_type=F32).astype(out_ref.dtype)


def route_rows(activations, block_ids, groups, tile=4096):
    rows, feat = activations.shape
    per = rows // groups
    return pl.pallas_call(
        _route_kernel,
        grid=(feat // tile,),
        in_specs=[
            pl.BlockSpec((rows, 1), lambda t: (0, 0)),
            pl.BlockSpec((1, rows), lambda t: (0, 0)),
            pl.BlockSpec((rows, tile), lambda t: (0, t)),
        ],
        out_specs=pl.BlockSpec((groups, per, tile), lambda t: (0, 0, t)),
        out_shape=jax.ShapeDtypeStruct((groups, per, feat), activations.dtype),
    )(block_ids, block_ids.reshape(1, rows), activations)


def fused_step(x, bias, enc, encb, dec, *, replicas, tile=4096, interpret=False):
    groups, _, feat = x.shape
    width = enc.shape[1]
    n_tiles = feat // tile
    chunk = feat // replicas
    kernel = functools.partial(_sae_kernel, n_tiles=n_tiles, tile=tile, chunk=chunk, replicas=replicas)

    def enc_map(p, t):
        return (t * (1 - p) + (n_tiles - 1) * p, 0)

    def dec_map(p, t):
        return (0, t * p)

    return pl.pallas_call(
        kernel,
        grid=(2, n_tiles),
        in_specs=[
            pl.BlockSpec(memory_space=pltpu.VMEM),
            pl.BlockSpec((1, tile), lambda p, t: (0, t)),
            pl.BlockSpec((tile, width), enc_map),
            pl.BlockSpec((1, width), lambda p, t: (0, 0)),
            pl.BlockSpec((width, tile), dec_map),
        ],
        out_specs=[
            pl.BlockSpec((2, groups, width), lambda p, t: (0, 0, 0)),
            pl.BlockSpec((replicas, width + 1, chunk), lambda p, t: (0, 0, 0)),
        ],
        out_shape=[
            jax.ShapeDtypeStruct((2, groups, width), BF16),
            jax.ShapeDtypeStruct((replicas, width + 1, chunk), BF16),
        ],
        scratch_shapes=[
            pltpu.VMEM((2, groups, width), F32),
            pltpu.VMEM((2, groups, width), BF16),
            pltpu.VMEM((2, width, groups), BF16),
            pltpu.VMEM((groups, tile), F32),
        ],
        compiler_params=pltpu.CompilerParams(
            dimension_semantics=("arbitrary", "arbitrary"),
            vmem_limit_bytes=48 * 1024 * 1024,
        ),
        interpret=interpret,
    )(x, bias.reshape(1, feat), enc, encb, dec)


def local(activations, block_ids, enc_weight, enc_bias, dec_weight, dec_bias):
    groups = lax.axis_size("latent")
    replicas = lax.axis_size("blk")
    tok_rows = activations.shape[0]
    features = activations.shape[1]
    width = enc_weight.shape[2]
    per_owner = tok_rows // groups
    block_of = block_ids[:, 0]
    matches = (block_of[:, None] == block_of[None, :]).astype(jnp.int32)
    earlier = jnp.sum(jnp.tril(matches, -1), axis=1)
    placed = block_of * per_owner + earlier
    outgoing = route_rows(activations, block_ids, groups)
    rows_block = tok_rows * replicas
    incoming = lax.all_to_all(outgoing, "latent", split_axis=0, concat_axis=0, tiled=True)
    codes, grad_rows = fused_step(
        incoming, dec_bias, enc_weight[0], enc_bias, dec_weight[0], replicas=replicas
    )
    gathered = lax.all_to_all(grad_rows, "blk", split_axis=0, concat_axis=0, tiled=True)
    summed = jnp.sum(gathered[:, :width, :].astype(F32), axis=0)
    blk_pieces = gathered[:, width, :3].reshape(1, 1, replicas * 3)
    loss_row = jnp.pad(blk_pieces, ((0, 0), (0, 0), (0, width - replicas * 3)))
    loss_row = jnp.broadcast_to(loss_row, (groups, 1, width))
    sendback = jnp.concatenate([codes.transpose(1, 0, 2), loss_row], axis=1)
    returned = lax.all_to_all(sendback, "latent", split_axis=0, concat_axis=0, tiled=True)
    token_codes = returned[:, :per_owner, :].reshape(tok_rows, width)[placed]
    summed_loss = jnp.sum(returned[:, per_owner, :].astype(F32))
    gradient = summed / rows_block
    loss_value = summed_loss / (tok_rows * groups * replicas * features)
    return (loss_value, token_codes, gradient[None])


def solution(mesh):
    placed = (
        P(("latent", "blk"), None),
        P(("latent", "blk"), None),
        P("latent", None, None),
        P("latent", None),
        P("latent", None, None),
        P(),
    )
    return jax.shard_map(
        local,
        mesh=mesh,
        in_specs=placed,
        out_specs=(P(), P(("latent", "blk"), None), P("latent", None, "blk")),
        check_vma=False,
    )
```
